32 devices in a mesh: dp: 4 (over y, x), expert: 8 (over z, core).
Axes of the slice: x: 2, y: 2, z: 4, core: 2. Of those that a mesh axis runs over, the one named last changes fastest.
Arguments:
- tokens_in: bfloat16 [4096, 2048], P(('dp', 'expert')), may hold values from -6 to 6
- cotangent: bfloat16 [4096, 2048], P(('dp', 'expert')), may hold values from -6 to 6
- router_prob: float32 [4096], P(('dp', 'expert')), may hold values from 0.1 to 1
- expert_ids: int32 [4096, 1], P(('dp', 'expert')), may hold values from 0 to 3; in each aligned block of 128 rows (0 to 127, 128 to 255, ...) at most 40 rows name the same one
- w_gate: bfloat16 [8, 2048, 384], P('expert'), may hold values from -0.125 to 0.125
- w_up: bfloat16 [8, 2048, 384], P('expert'), may hold values from -0.125 to 0.125
- w_down: bfloat16 [8, 384, 2048], P('expert'), may hold values from -0.21875 to 0.21875
Outputs:
- layer_out: bfloat16 [4096, 2048], P(('dp', 'expert'))
- grad_input: bfloat16 [4096, 2048], P(('dp', 'expert'))
- grad_w_down: bfloat16 [8, 384, 2048], P('expert', 'dp')
The draws below stay inside these ranges and needn't reach their ends.
Inputs may be any that keep to these rules, and one draw needn't show every extreme that they name: `expert_ids`: among the 128 tokens of one device no expert id appears more than 40 times.
All inputs are finite; a program needn't handle non-finite values.
Results may differ from the reference program's by a relative error of at most 0.012.
Values may be sent and summed in bfloat16 or wider, within the bound.
No kernel may reach another device: no remote copies, remote signals or barrier semaphores. Data moves between devices by JAX's collectives and lax.ppermute only.
A program may use at most 64 MiB of HBM per device.

```python
import math
import jax
import jax.numpy as jnp
import numpy as np
from jax import lax

D = 2048
FF = 768
TOP = 1
TOK_DEV = 128
EXPERTS = 4
MOST = 40
TOKENS = 4096
N_DP = 4
N_EXPERT = 8


def steps_of(rng, shape, shards, low, high):
    def one(position, parts):
        heights = jax.random.uniform(jax.random.fold_in(jax.random.fold_in(rng, 6), position), (parts,), jnp.float32, low / len(shards), high / len(shards))
        return jnp.repeat(jnp.exp(heights), shape[position] // parts).reshape((-1,) + (1,) * (len(shape) - position - 1))

    loudness = one(*shards[0])
    for cut in shards[1:]:
        loudness = loudness * one(*cut)
    return loudness


def deal_out(stream_key, own, number, rows, count, top, most, slope):
    sequence = jax.random.permutation(stream_key, count)
    heavy_load, common = load_shares(count, rows * top, most, slope, True), load_shares(count, rows * top, most, slope, False)
    places = jnp.arange(count)

    def named(sizes, rotation):
        used = int((sizes > 0).sum())
        fixed = max(1, used // 4)
        passed = fixed + (places - fixed + rotation * (used - fixed)) % max(1, count - fixed)
        return jnp.zeros((count,), jnp.int32).at[sequence[jnp.where(places < fixed, places, passed)]].set(jnp.asarray(sizes, jnp.int32))

    sizes = jnp.where(number % 4 == 0, named(heavy_load, number // 4), named(common, number - number // 4 - 1))
    mixed = jax.random.permutation(jax.random.fold_in(own, 3), count)
    giver, sink = mixed[0:count // 2 * 2:2], mixed[1:count // 2 * 2:2]
    slack = jnp.minimum(sizes[giver] - 1, most - sizes[sink]) // 2
    slack = jnp.where((giver == sequence[0]) | (sink == sequence[0]) | (sizes[sink] == 0), 0, jnp.maximum(slack, 0))
    passed = jax.random.randint(jax.random.fold_in(own, 4), (count // 2,), 0, 1 << 20) % (slack + 1)
    sizes = sizes.at[giver].add(-passed).at[sink].add(passed)
    items = jnp.searchsorted(jnp.cumsum(sizes), jnp.arange(rows * top), side="right").astype(jnp.int32)
    grid = items.reshape(top, rows).T
    grid = grid[jax.random.permutation(jax.random.fold_in(own, 1), rows)]
    rotation = jax.random.randint(jax.random.fold_in(own, 2), (rows, 1), 0, top)
    return jnp.take_along_axis(grid, (jnp.arange(top)[None, :] + rotation) % top, axis=1)


def load_shares(amount, total, most, lean, full):
    portions = [(1 << 20) // math.isqrt(grade ** lean) + 1 for grade in range(1, amount + 1)]
    largest = most if full else min(most, max(-(-total // amount), total * portions[0] // sum(portions)))
    least = 1 if total - largest >= amount - 1 else 0
    given, surplus = [largest] + [least] * (amount - 1), total - largest - least * (amount - 1)
    while surplus > 0:
        candidates = [i for i in range(1, amount) if given[i] < largest] or [i for i in range(1, amount) if given[i] < most]
        pool, remaining = sum([portions[i] for i in candidates]), surplus
        for i in candidates:
            addition = min(most - given[i], max(1, remaining * portions[i] // pool), surplus)
            given[i] = given[i] + addition
            surplus = surplus - addition
    return np.array(given)


def bell_draw(key, dims, scale, limit, pieces=(), kind=jnp.bfloat16):
    factor_of = steps_of(key, dims, pieces, -0.22, 0.18) if pieces else 1.0
    array = jax.random.normal(key, dims, jnp.float32) * scale * factor_of
    return jnp.minimum(jnp.maximum(array, -limit), limit).astype(kind)


def setup_inputs(seed: int = 0) -> dict:
    key_of = jax.random.split(jax.random.key(seed), 8)
    tokens_in = bell_draw(key_of[0], (TOKENS, D), 1.0, 6.0, ((0, 32),))
    cotangent = bell_draw(key_of[1], (TOKENS, D), 1.0, 6.0, ((0, 32),))
    router_prob = jnp.clip(jnp.exp(math.log(1.0) - 2.3025851 * jax.random.uniform(key_of[2], (TOKENS,), jnp.float32) ** steps_of(key_of[2], (TOKENS,), ((0, 32),), -0.2, 0.2)), 0.1, 1.0)
    expert_ids_keys = jax.random.split(jax.random.fold_in(key_of[3], 1), TOKENS // TOK_DEV)
    expert_ids_turns = jax.random.permutation(jax.random.fold_in(key_of[3], 3), TOKENS // TOK_DEV)
    expert_ids = jax.vmap(lambda own, number: deal_out(jax.random.fold_in(key_of[3], 2), own, number, TOK_DEV, EXPERTS, TOP, MOST, 1))(expert_ids_keys, expert_ids_turns).reshape((TOKENS, TOP))
    w_gate = bell_draw(key_of[4], (2 * EXPERTS, D, FF // 2), D ** -0.5, 0.125, ((0, 8),))
    w_up = bell_draw(key_of[5], (2 * EXPERTS, D, FF // 2), D ** -0.5, 0.125, ((0, 8),))
    w_down = bell_draw(key_of[6], (2 * EXPERTS, FF // 2, D), FF ** -0.5, 0.21875, ((0, 8),))
    return dict(tokens_in=tokens_in, cotangent=cotangent, router_prob=router_prob, expert_ids=expert_ids, w_gate=w_gate, w_up=w_up, w_down=w_down)


def round_trip(value):
    return lax.optimization_barrier(value.astype(jnp.bfloat16)).astype(jnp.float32)


def reference(tokens_in, cotangent, router_prob, expert_ids, w_gate, w_up, w_down):
    experts = EXPERTS
    half_units = FF // 2
    devices = N_DP * N_EXPERT
    ids = expert_ids[:, 0].reshape(devices, TOK_DEV)
    columns = jnp.arange(experts, dtype=jnp.int32)
    onehot = (ids[:, :, None] == columns[None, None, :]).astype(jnp.int32)
    rank = jnp.sum((jnp.cumsum(onehot, axis=1) - onehot) * onehot, axis=2).astype(jnp.int32)
    source = jnp.arange(devices, dtype=jnp.int32)[:, None]
    flat = ((ids * devices + source) * MOST + rank).reshape(-1).astype(jnp.int32)
    scaled = (router_prob[:, None] * cotangent.astype(jnp.float32)).astype(jnp.bfloat16)
    total_slots = experts * devices * MOST
    rows_x = jnp.zeros((total_slots, D), jnp.bfloat16).at[flat].set(tokens_in).reshape(experts, devices * MOST, D)
    rows_dy = jnp.zeros((total_slots, D), jnp.bfloat16).at[flat].set(scaled).reshape(experts, devices * MOST, D)
    gate_full = w_gate.reshape(experts, 2, D, half_units).transpose(0, 2, 1, 3).reshape(experts, D, FF)
    up_full = w_up.reshape(experts, 2, D, half_units).transpose(0, 2, 1, 3).reshape(experts, D, FF)
    down_full = w_down.reshape(experts, FF, D)
    contract = (((1,), (1,)), ((), ()))

    def per_expert(packed):
        xrows, dyrows, g_w, u_w, d_w = packed
        gate = jnp.dot(xrows, g_w, preferred_element_type=jnp.float32)
        upval = jnp.dot(xrows, u_w, preferred_element_type=jnp.float32)
        sig = jax.nn.sigmoid(gate)
        active = gate * sig
        hidden = (active * upval).astype(jnp.bfloat16)
        out_lower = jnp.dot(hidden[:, :half_units], d_w[:half_units], preferred_element_type=jnp.float32)
        out_upper = jnp.dot(hidden[:, half_units:], d_w[half_units:], preferred_element_type=jnp.float32)
        outrows = (round_trip(out_lower) + round_trip(out_upper)).astype(jnp.bfloat16)
        grad_hidden = lax.dot_general(dyrows, d_w, contract, preferred_element_type=jnp.float32)
        grad_gate = (grad_hidden * upval * sig * (1.0 + gate * (1.0 - sig))).astype(jnp.bfloat16)
        grad_up = (grad_hidden * active).astype(jnp.bfloat16)
        grad_lower = lax.dot_general(grad_gate[:, :half_units], g_w[:, :half_units], contract, preferred_element_type=jnp.float32)
        grad_lower = grad_lower + lax.dot_general(grad_up[:, :half_units], u_w[:, :half_units], contract, preferred_element_type=jnp.float32)
        grad_higher = lax.dot_general(grad_gate[:, half_units:], g_w[:, half_units:], contract, preferred_element_type=jnp.float32)
        grad_higher = grad_higher + lax.dot_general(grad_up[:, half_units:], u_w[:, half_units:], contract, preferred_element_type=jnp.float32)
        grad_rows = (round_trip(grad_lower) + round_trip(grad_higher)).astype(jnp.bfloat16)
        hidden_groups = hidden.reshape(N_DP, N_EXPERT * MOST, FF).astype(jnp.float32)
        dy_groups = dyrows.reshape(N_DP, N_EXPERT * MOST, D).astype(jnp.float32)
        terms = jnp.einsum("gri,grd->gid", hidden_groups, dy_groups).astype(jnp.bfloat16)
        weight_grad = jnp.sum(terms.astype(jnp.float32), axis=0).astype(jnp.bfloat16)
        return outrows, grad_rows, weight_grad

    outs, grads, weight_grads = lax.map(per_expert, (rows_x, rows_dy, gate_full, up_full, down_full))
    out_tok = outs.reshape(-1, D)[flat]
    grad_input = grads.reshape(-1, D)[flat]
    layer_out = (router_prob[:, None] * out_tok.astype(jnp.float32)).astype(jnp.bfloat16)
    grad_w_down = weight_grads.reshape(2 * experts, half_units, D)
    return layer_out, grad_input, grad_w_down
```

```python
import functools

import jax
import jax.numpy as jnp
from jax import lax
from jax.experimental import pallas as pl
from jax.experimental.pallas import tpu as pltpu
from jax.sharding import PartitionSpec as P


NN = (((1,), (0,)), ((), ()))
NT = (((1,), (1,)), ((), ()))
TN = (((0,), (0,)), ((), ()))


def dot(a, b, dims=NN):
    return lax.dot_general(a, b, dims, preferred_element_type=jnp.float32)


def swap(block, axis, mask):
    route = [(i, i ^ mask) for i in range(lax.axis_size(axis))]
    return lax.ppermute(block, axis, route)


def slots_of(ids, chips, block):
    tok = ids.shape[1]
    chip = lax.axis_index("expert") // 2
    ranks = -(-chips // 8) * 8
    apart = jnp.bitwise_xor(ids, chip)
    match = lax.broadcasted_iota(jnp.int32, (ranks, tok), 0) == apart
    onehot = match.astype(jnp.float32)
    earlier = lax.broadcasted_iota(jnp.int32, (tok, tok), 0) < lax.broadcasted_iota(
        jnp.int32, (tok, tok), 1
    )
    before = dot(onehot.astype(jnp.bfloat16), earlier.astype(jnp.float32).astype(jnp.bfloat16))
    rank = jnp.sum(before * onehot, axis=0, keepdims=True).astype(jnp.int32)
    return apart * block + rank


def column_of(row):
    tok = row.shape[1]
    eye = lax.broadcasted_iota(jnp.int32, (tok, tok), 0) == lax.broadcasted_iota(
        jnp.int32, (tok, tok), 1
    )
    return jnp.sum(jnp.where(eye, row, 0.0), axis=1, keepdims=True)


def dispatch_body(chips, block, ids_ref, prob_ref, x_ref, dy_ref, *out_refs):
    tok = x_ref.shape[0]
    slot = slots_of(ids_ref[...], chips, block)
    rows = chips * block
    placing = (lax.broadcasted_iota(jnp.int32, (rows, tok), 0) == slot).astype(jnp.float32)
    placing = placing.astype(jnp.bfloat16)
    scaled = (column_of(prob_ref[...]) * dy_ref[...].astype(jnp.float32)).astype(jnp.bfloat16)
    send_x = dot(placing, x_ref[...])
    send_dy = dot(placing, scaled)
    for j in range(chips):
        out_refs[j][:block, :] = send_x[j * block : (j + 1) * block].astype(jnp.bfloat16)
        out_refs[j][block:, :] = send_dy[j * block : (j + 1) * block].astype(jnp.bfloat16)


def combine_body(chips, block, ids_ref, prob_ref, *refs):
    back, (out_ref, grad_ref) = refs[:chips], refs[chips:]
    tok = out_ref.shape[0]
    slot = slots_of(ids_ref[...], chips, block)
    rows = chips * block
    placing = (lax.broadcasted_iota(jnp.int32, (rows, tok), 0) == slot).astype(jnp.float32)
    placing = placing.astype(jnp.bfloat16)
    out = jnp.concatenate([ref[:block, :] for ref in back], axis=0)
    grad = jnp.concatenate([ref[block:, :] for ref in back], axis=0)
    out_ref[...] = (column_of(prob_ref[...]) * dot(placing, out, TN)).astype(jnp.bfloat16)
    grad_ref[...] = dot(placing, grad, TN).astype(jnp.bfloat16)


def expert_body(count, block, *refs):
    chunks, refs = refs[:count], refs[count:]
    own, other, refs = refs[:3], refs[3:6], refs[6:]
    backs, (kept_ref, shared_ref), refs = refs[:count], refs[count : count + 2], refs[count + 2 :]
    x, dy, out, grad = refs
    model = x.shape[1]
    tile = own[0].shape[2]
    step = pl.program_id(0)

    @pl.when(step == 0)
    def _():
        for n in range(count):
            x[n * block : (n + 1) * block, :] = chunks[n][:block, :]
            dy[n * block : (n + 1) * block, :] = chunks[n][block:, :]
        shared_ref[:, :model] = dy[...]
        out[...] = jnp.zeros_like(out)
        grad[...] = jnp.zeros_like(grad)

    for half, (gate_w, up_w, down_w) in enumerate((own, other)):
        gate = dot(x[...], gate_w[0])
        up = dot(x[...], up_w[0])
        sig = jax.nn.sigmoid(gate)
        active = gate * sig
        hidden = (active * up).astype(jnp.bfloat16)
        if half == 0:
            kept_ref[...] = hidden
        else:
            shared_ref[:, pl.ds(pl.multiple_of(model + step * tile, tile), tile)] = hidden
        out[...] += dot(hidden, down_w[0])
        grad_hidden = dot(dy[...], down_w[0], NT)
        grad_gate = (grad_hidden * up * sig * (1.0 + gate * (1.0 - sig))).astype(jnp.bfloat16)
        grad_up = (grad_hidden * active).astype(jnp.bfloat16)
        grad[...] += dot(grad_gate, gate_w[0], NT) + dot(grad_up, up_w[0], NT)

    @pl.when(step == pl.num_programs(0) - 1)
    def _():
        for n in range(count):
            backs[n][:block, :] = out[n * block : (n + 1) * block, :].astype(jnp.bfloat16)
            backs[n][block:, :] = grad[n * block : (n + 1) * block, :].astype(jnp.bfloat16)


def expert(chunks, own, other):
    count = len(chunks)
    block, model = chunks[0].shape[0] // 2, chunks[0].shape[1]
    units = own[0].shape[2]
    tile = 128
    rows = count * block
    whole = pl.BlockSpec((2 * block, model), lambda i: (0, 0))
    wide = pl.BlockSpec((1, model, tile), lambda i: (0, 0, i))
    tall = pl.BlockSpec((1, tile, model), lambda i: (0, i, 0))
    results = pl.pallas_call(
        functools.partial(expert_body, count, block),
        grid=(units // tile,),
        in_specs=[whole] * count + [wide, wide, tall] * 2,
        out_specs=[whole] * count
        + [
            pl.BlockSpec((rows, tile), lambda i: (0, i)),
            pl.BlockSpec((rows, model + units), lambda i: (0, 0)),
        ],
        out_shape=[jax.ShapeDtypeStruct((2 * block, model), jnp.bfloat16)] * count
        + [
            jax.ShapeDtypeStruct((rows, units), jnp.bfloat16),
            jax.ShapeDtypeStruct((rows, model + units), jnp.bfloat16),
        ],
        scratch_shapes=[
            pltpu.VMEM((rows, model), jnp.bfloat16),
            pltpu.VMEM((rows, model), jnp.bfloat16),
            pltpu.VMEM((rows, model), jnp.float32),
            pltpu.VMEM((rows, model), jnp.float32),
        ],
        compiler_params=pltpu.CompilerParams(vmem_limit_bytes=32 << 20),
        cost_estimate=pl.CostEstimate(
            flops=24 * rows * model * units,
            bytes_accessed=12 * model * units + 8 * rows * model,
            transcendentals=2 * rows * units,
        ),
        name="expert",
    )(*chunks, *own, *other)
    return results[:count], results[count], results[count + 1]


def weight_body(chunk_count, groups, block, parts, *refs):
    chunks, kept = refs[:chunk_count], refs[chunk_count : chunk_count + groups]
    shared = refs[chunk_count + groups : chunk_count + 2 * groups]
    outs, term = refs[chunk_count + 2 * groups : -1], refs[-1]
    columns = term.shape[1]
    model = chunks[0].shape[1]
    here = pl.ds(pl.multiple_of(pl.program_id(0) * columns, columns), columns)
    hidden = jnp.concatenate(
        [ref[...] for ref in kept] + [ref[:, model:] for ref in shared], axis=0
    )
    dy = jnp.concatenate(
        [ref[block:, here] for ref in chunks] + [ref[:, here] for ref in shared], axis=0
    )
    term[...] = dot(hidden, dy, TN)
    if parts == 1:
        outs[0][...] = term[...].astype(jnp.bfloat16)
        return
    me = lax.axis_index("dp")
    height = term.shape[0] // parts
    for m in range(parts):
        first = pl.multiple_of(jnp.bitwise_xor(me, m) * height, 8)
        outs[m][...] = term[pl.ds(first, height), :].astype(jnp.bfloat16)


def weight_terms(chunks, kept, shared, parts):
    block, model = chunks[0].shape[0] // 2, chunks[0].shape[1]
    units = kept[0].shape[1]
    columns = 512
    full = lambda a: pl.BlockSpec(a.shape, lambda i: (0, 0))
    rows = 2 * sum(a.shape[0] for a in kept)
    return pl.pallas_call(
        functools.partial(weight_body, len(chunks), len(kept), block, parts),
        grid=(model // columns,),
        in_specs=[full(a) for a in (*chunks, *kept, *shared)],
        out_specs=[pl.BlockSpec((units // parts, columns), lambda i: (0, i))] * parts,
        out_shape=[jax.ShapeDtypeStruct((units // parts, model), jnp.bfloat16)] * parts,
        scratch_shapes=[pltpu.VMEM((units, columns), jnp.float32)],
        compiler_params=pltpu.CompilerParams(vmem_limit_bytes=24 << 20),
        cost_estimate=pl.CostEstimate(
            flops=2 * rows * model * units,
            bytes_accessed=2 * (rows * (model + units) + units * model),
            transcendentals=0,
        ),
        name="weight_terms",
    )(*chunks, *kept, *shared)


def per_device(tokens_in, cotangent, router_prob, expert_ids, w_gate, w_up, w_down):
    chips = lax.axis_size("expert") // 2
    tok, model = tokens_in.shape
    most = 5 * tok // (4 * chips)
    block = -(-most // 8) * 8
    ids = expert_ids.reshape(1, tok)
    prob = router_prob.reshape(1, tok)
    sends = pl.pallas_call(
        functools.partial(dispatch_body, chips, block),
        out_shape=[jax.ShapeDtypeStruct((2 * block, model), jnp.bfloat16)] * chips,
        compiler_params=pltpu.CompilerParams(vmem_limit_bytes=16 << 20),
        cost_estimate=pl.CostEstimate(
            flops=4 * chips * block * tok * model,
            bytes_accessed=4 * (chips * block + tok) * model,
            transcendentals=0,
        ),
        name="dispatch",
    )(ids, prob, tokens_in, cotangent)
    own = (w_gate, w_up, w_down)
    order = sorted(range(1, chips), key=lambda j: -(j.bit_length()))
    order = sorted(order, key=lambda j: (j < 2, j))
    arrived = {0: sends[0]}
    for j in order:
        arrived[j] = swap(sends[j], "expert", 2 * j)
    other = tuple(swap(w, "expert", 1) for w in own)
    each = max(1, chips // 4)
    groups = [list(range(g, g + each)) for g in range(0, chips, each)]
    if len(groups) > 1:
        groups = [groups[0] + groups[1]] + groups[2:]
    kept, shared, backs = [], [], {}
    for group in groups:
        results, mine, theirs = expert([arrived[j] for j in group], own, other)
        for j, result in zip(group, results):
            backs[j] = swap(result, "expert", 2 * j) if j else result
        kept.append(mine)
        shared.append(swap(theirs, "expert", 1))
    parts = lax.axis_size("dp")
    units = w_down.shape[1]
    direct = parts <= 8 and units % (8 * parts) == 0
    terms = weight_terms([arrived[j] for g in groups for j in g], kept, shared, parts if direct else 1)
    if direct:
        total = terms[0].astype(jnp.float32)
        for m in range(1, parts):
            total = total + swap(terms[m], "dp", m).astype(jnp.float32)
        summed = total.astype(jnp.bfloat16)
    else:
        summed = lax.psum_scatter(terms[0], "dp", scatter_dimension=0, tiled=True)
    layer_out, grad_input = pl.pallas_call(
        functools.partial(combine_body, chips, block),
        out_shape=[jax.ShapeDtypeStruct((tok, model), jnp.bfloat16)] * 2,
        compiler_params=pltpu.CompilerParams(vmem_limit_bytes=16 << 20),
        cost_estimate=pl.CostEstimate(
            flops=4 * chips * block * tok * model,
            bytes_accessed=4 * (chips * block + tok) * model,
            transcendentals=0,
        ),
        name="combine",
    )(ids, prob, *[backs[j] for j in range(chips)])
    return layer_out, grad_input, summed[None]


def solution(mesh):
    placed = (
        P(("dp", "expert"), None),
        P(("dp", "expert"), None),
        P(("dp", "expert")),
        P(("dp", "expert"), None),
        P("expert", None, None),
        P("expert", None, None),
        P("expert", None, None),
    )
    return jax.shard_map(
        per_device,
        mesh=mesh,
        in_specs=placed,
        out_specs=(P(("dp", "expert"), None), P(("dp", "expert"), None), P("expert", "dp", None)),
        check_vma=False,
    )
```

```python
import functools

import jax
import jax.numpy as jnp
from jax import lax
from jax.experimental import pallas as pl
from jax.experimental.pallas import tpu as pltpu
from jax.sharding import PartitionSpec as P


NN = (((1,), (0,)), ((), ()))
NT = (((1,), (1,)), ((), ()))
TN = (((0,), (0,)), ((), ()))


def dot(a, b, dims=NN):
    return lax.dot_general(a, b, dims, preferred_element_type=jnp.float32)


def in_hbm(array):
    return pltpu.with_memory_space_constraint(array, pltpu.HBM)


def swap(block, axis, mask):
    route = [(i, i ^ mask) for i in range(lax.axis_size(axis))]
    return lax.ppermute(block, axis, route)


def slots_of(ids, chips, block):
    tok = ids.shape[1]
    chip = lax.axis_index("expert") // 2
    ranks = -(-chips // 8) * 8
    apart = jnp.bitwise_xor(ids, chip)
    match = lax.broadcasted_iota(jnp.int32, (ranks, tok), 0) == apart
    onehot = match.astype(jnp.float32)
    earlier = lax.broadcasted_iota(jnp.int32, (tok, tok), 0) < lax.broadcasted_iota(
        jnp.int32, (tok, tok), 1
    )
    before = dot(onehot.astype(jnp.bfloat16), earlier.astype(jnp.float32).astype(jnp.bfloat16))
    rank = jnp.sum(before * onehot, axis=0, keepdims=True).astype(jnp.int32)
    return apart * block + rank


def column_of(row):
    tok = row.shape[1]
    eye = lax.broadcasted_iota(jnp.int32, (tok, tok), 0) == lax.broadcasted_iota(
        jnp.int32, (tok, tok), 1
    )
    return jnp.sum(jnp.where(eye, row, 0.0), axis=1, keepdims=True)


def dispatch_body(chips, block, *refs):
    sources, out_refs, held, sems = refs[:4], refs[4 : 4 + chips], refs[4 + chips : -1], refs[-1]
    fetches = [pltpu.make_async_copy(sources[n], held[n], sems.at[n]) for n in range(4)]
    for fetch in fetches:
        fetch.start()
    ids_ref, prob_ref, x_ref, dy_ref = held
    fetch_x, fetch_dy = fetches[2:]
    fetches[0].wait()
    fetches[1].wait()
    tok = x_ref.shape[0]
    slot = slots_of(ids_ref[...], chips, block)
    rows = chips * block
    placing = (lax.broadcasted_iota(jnp.int32, (rows, tok), 0) == slot).astype(jnp.float32)
    placing = placing.astype(jnp.bfloat16)
    column = column_of(prob_ref[...])
    fetch_x.wait()
    send_x = dot(placing, x_ref[...]).astype(jnp.bfloat16)
    for j in range(chips):
        out_refs[j][:block, :] = send_x[j * block : (j + 1) * block]
    fetch_dy.wait()
    scaled = (column * dy_ref[...].astype(jnp.float32)).astype(jnp.bfloat16)
    send_dy = dot(placing, scaled).astype(jnp.bfloat16)
    for j in range(chips):
        out_refs[j][block:, :] = send_dy[j * block : (j + 1) * block]


def stage_body(*refs):
    count = len(refs) // 2
    sems = refs[-1]
    copies = [pltpu.make_async_copy(refs[n], refs[count + n], sems.at[n]) for n in range(count)]
    for copy in copies:
        copy.start()
    for copy in copies:
        copy.wait()


def stage(arrays):
    return pl.pallas_call(
        stage_body,
        in_specs=[pl.BlockSpec(memory_space=pltpu.HBM)] * len(arrays),
        out_specs=[pl.BlockSpec(memory_space=pltpu.VMEM)] * len(arrays),
        out_shape=[pltpu.VMEM(a.shape, a.dtype) for a in arrays],
        scratch_shapes=[pltpu.SemaphoreType.DMA((len(arrays),))],
        compiler_params=pltpu.CompilerParams(vmem_limit_bytes=8 << 20),
        cost_estimate=pl.CostEstimate(
            flops=0, bytes_accessed=sum(4 * a.size for a in arrays), transcendentals=0
        ),
        name="stage",
    )(*[in_hbm(a) for a in arrays])


def combine_body(chips, block, ids_ref, prob_ref, *refs):
    back, (out_ref, grad_ref) = refs[:chips], refs[chips:]
    tok = out_ref.shape[0]
    slot = slots_of(ids_ref[...], chips, block)
    rows = chips * block
    placing = (lax.broadcasted_iota(jnp.int32, (rows, tok), 0) == slot).astype(jnp.float32)
    placing = placing.astype(jnp.bfloat16)
    out = jnp.concatenate([ref[:block, :] for ref in back], axis=0)
    grad = jnp.concatenate([ref[block:, :] for ref in back], axis=0)
    out_ref[...] = (column_of(prob_ref[...]) * dot(placing, out, TN)).astype(jnp.bfloat16)
    grad_ref[...] = dot(placing, grad, TN).astype(jnp.bfloat16)


def expert_body(count, block, tile, *refs):
    chunks, refs = refs[:count], refs[count:]
    own, other, refs = refs[:3], refs[3:6], refs[6:]
    backs, (kept_ref, shared_ref, out, grad) = refs[:count], refs[count:]
    model = chunks[0].shape[1]
    units = kept_ref.shape[1]
    x = jnp.concatenate([ref[:block, :] for ref in chunks], axis=0)
    dy = jnp.concatenate([ref[block:, :] for ref in chunks], axis=0)
    shared_ref[:, :model] = dy
    for first in range(0, units, tile):
        part = slice(first, first + tile)
        gate_w, up_w = (
            jnp.concatenate([own[n][0, :, part], other[n][0, :, part]], axis=1) for n in (0, 1)
        )
        down_w = jnp.concatenate([own[2][0, part, :], other[2][0, part, :]], axis=0)
        gate = dot(x, gate_w)
        up = dot(x, up_w)
        grad_hidden = dot(dy, down_w, NT)
        sig = jax.nn.sigmoid(gate)
        active = gate * sig
        hidden = (active * up).astype(jnp.bfloat16)
        kept_ref[:, part] = hidden[:, :tile]
        shared_ref[:, model + first : model + first + tile] = hidden[:, tile:]
        grad_gate = (grad_hidden * up * sig * (1.0 + gate * (1.0 - sig))).astype(jnp.bfloat16)
        grad_up = (grad_hidden * active).astype(jnp.bfloat16)
        new_out = dot(hidden, down_w)
        new_grad = dot(grad_gate, gate_w, NT) + dot(grad_up, up_w, NT)
        if first:
            new_out, new_grad = out[...] + new_out, grad[...] + new_grad
        if first + tile < units:
            out[...], grad[...] = new_out, new_grad
            continue
        for n in range(count):
            backs[n][:block, :] = new_out[n * block : (n + 1) * block, :].astype(jnp.bfloat16)
            backs[n][block:, :] = new_grad[n * block : (n + 1) * block, :].astype(jnp.bfloat16)


def expert(chunks, own, other):
    count = len(chunks)
    block, model = chunks[0].shape[0] // 2, chunks[0].shape[1]
    units = own[0].shape[2]
    rows = count * block
    vmem = pl.BlockSpec(memory_space=pltpu.VMEM)
    results = pl.pallas_call(
        functools.partial(expert_body, count, block, 128),
        in_specs=[vmem] * (count + 6),
        out_specs=[vmem] * (count + 2),
        out_shape=[jax.ShapeDtypeStruct((2 * block, model), jnp.bfloat16)] * count
        + [
            jax.ShapeDtypeStruct((rows, units), jnp.bfloat16),
            jax.ShapeDtypeStruct((rows, model + units), jnp.bfloat16),
        ],
        scratch_shapes=[
            pltpu.VMEM((rows, model), jnp.float32),
            pltpu.VMEM((rows, model), jnp.float32),
        ],
        compiler_params=pltpu.CompilerParams(vmem_limit_bytes=28 << 20),
        cost_estimate=pl.CostEstimate(
            flops=24 * rows * model * units,
            bytes_accessed=12 * model * units + 8 * rows * model,
            transcendentals=2 * rows * units,
        ),
        name="expert",
    )(*chunks, *own, *other)
    return results[:count], results[count], results[count + 1]


def weight_body(chunk_count, groups, block, parts, *refs):
    chunks, kept = refs[:chunk_count], refs[chunk_count : chunk_count + groups]
    shared = refs[chunk_count + groups : chunk_count + 2 * groups]
    outs, term = refs[chunk_count + 2 * groups : -1], refs[-1]
    columns = term.shape[1]
    model = chunks[0].shape[1]
    here = pl.ds(pl.multiple_of(pl.program_id(0) * columns, columns), columns)
    hidden = jnp.concatenate(
        [ref[...] for ref in kept] + [ref[:, model:] for ref in shared], axis=0
    )
    dy = jnp.concatenate(
        [ref[block:, here] for ref in chunks] + [ref[:, here] for ref in shared], axis=0
    )
    term[...] = dot(hidden, dy, TN)
    if parts == 1:
        outs[0][...] = term[...].astype(jnp.bfloat16)
        return
    me = lax.axis_index("dp")
    height = term.shape[0] // parts
    for m in range(parts):
        first = pl.multiple_of(jnp.bitwise_xor(me, m) * height, 8)
        outs[m][...] = term[pl.ds(first, height), :].astype(jnp.bfloat16)


def weight_terms(chunks, kept, shared, parts):
    block, model = chunks[0].shape[0] // 2, chunks[0].shape[1]
    units = kept[0].shape[1]
    columns = 512
    full = lambda a: pl.BlockSpec(a.shape, lambda i: (0, 0))
    rows = 2 * sum(a.shape[0] for a in kept)
    return pl.pallas_call(
        functools.partial(weight_body, len(chunks), len(kept), block, parts),
        grid=(model // columns,),
        in_specs=[full(a) for a in (*chunks, *kept, *shared)],
        out_specs=[pl.BlockSpec((units // parts, columns), lambda i: (0, i))] * parts,
        out_shape=[jax.ShapeDtypeStruct((units // parts, model), jnp.bfloat16)] * parts,
        scratch_shapes=[pltpu.VMEM((units, columns), jnp.float32)],
        compiler_params=pltpu.CompilerParams(vmem_limit_bytes=16 << 20),
        cost_estimate=pl.CostEstimate(
            flops=2 * rows * model * units,
            bytes_accessed=2 * (rows * (model + units) + units * model),
            transcendentals=0,
        ),
        name="weight_terms",
    )(*chunks, *kept, *shared)


def plan(chips):
    each = max(1, chips // 4)
    groups = [list(range(g, g + each)) for g in range(0, chips, each)]
    if len(groups) > 1:
        groups = groups[:2:-1] + [groups[0] + groups[1]] + groups[2:3]
    return [j for group in groups for j in group if j], groups


def direct_sum(parts, units):
    return parts <= 8 and units % (8 * parts) == 0


def per_device(tokens_in, cotangent, router_prob, expert_ids, w_gate, w_up, w_down):
    chips = lax.axis_size("expert") // 2
    tok, model = tokens_in.shape
    most = 5 * tok // (4 * chips)
    block = -(-most // 8) * 8
    ids = expert_ids.reshape(1, tok)
    prob = router_prob.reshape(1, tok)
    sends = pl.pallas_call(
        functools.partial(dispatch_body, chips, block),
        in_specs=[pl.BlockSpec(memory_space=pltpu.HBM)] * 4,
        out_shape=[jax.ShapeDtypeStruct((2 * block, model), jnp.bfloat16)] * chips,
        scratch_shapes=[
            pltpu.VMEM((1, tok), jnp.int32),
            pltpu.VMEM((1, tok), jnp.float32),
            pltpu.VMEM((tok, model), jnp.bfloat16),
            pltpu.VMEM((tok, model), jnp.bfloat16),
            pltpu.SemaphoreType.DMA((4,)),
        ],
        compiler_params=pltpu.CompilerParams(vmem_limit_bytes=16 << 20),
        cost_estimate=pl.CostEstimate(
            flops=4 * chips * block * tok * model,
            bytes_accessed=4 * (chips * block + tok) * model,
            transcendentals=0,
        ),
        name="dispatch",
    )(*[in_hbm(a) for a in (ids, prob, tokens_in, cotangent)])
    own = (w_gate, w_up, w_down)
    order, groups = plan(chips)
    arrived = {0: sends[0]}
    for j in order:
        arrived[j] = swap(sends[j], "expert", 2 * j)
    other = tuple(swap(w, "expert", 1) for w in own)
    own = stage(own)
    kept, shared, backs = [], [], {}
    for group in groups:
        results, mine, theirs = expert([arrived[j] for j in group], own, other)
        for j, result in zip(group, results):
            backs[j] = swap(result, "expert", 2 * j) if j else result
        kept.append(mine)
        shared.append(swap(theirs, "expert", 1))
    parts = lax.axis_size("dp")
    direct = direct_sum(parts, w_down.shape[1])
    rows = [arrived[j] for group in groups for j in group]
    terms = weight_terms(rows, kept, shared, parts if direct else 1)
    if direct:
        total = terms[0].astype(jnp.float32)
        for m in range(1, parts):
            total = total + swap(terms[m], "dp", m).astype(jnp.float32)
        summed = total.astype(jnp.bfloat16)
    else:
        summed = lax.psum_scatter(terms[0], "dp", scatter_dimension=0, tiled=True)
    layer_out, grad_input = pl.pallas_call(
        functools.partial(combine_body, chips, block),
        out_shape=[jax.ShapeDtypeStruct((tok, model), jnp.bfloat16)] * 2,
        compiler_params=pltpu.CompilerParams(vmem_limit_bytes=16 << 20),
        cost_estimate=pl.CostEstimate(
            flops=4 * chips * block * tok * model,
            bytes_accessed=4 * (chips * block + tok) * model,
            transcendentals=0,
        ),
        name="combine",
    )(ids, prob, *[backs[j] for j in range(chips)])
    return layer_out, grad_input, summed[None]


def solution(mesh):
    placed = (
        P(("dp", "expert"), None),
        P(("dp", "expert"), None),
        P(("dp", "expert")),
        P(("dp", "expert"), None),
        P("expert", None, None),
        P("expert", None, None),
        P("expert", None, None),
    )

    return jax.shard_map(
        per_device,
        mesh=mesh,
        in_specs=placed,
        out_specs=(P(("dp", "expert"), None), P(("dp", "expert"), None), P("expert", "dp", None)),
        check_vma=False,
    )
```

```python
import functools

import jax
import jax.numpy as jnp
from jax import lax
from jax.experimental import pallas as pl
from jax.experimental.pallas import tpu as pltpu
from jax.sharding import PartitionSpec as P


NN = (((1,), (0,)), ((), ()))
NT = (((1,), (1,)), ((), ()))
TN = (((0,), (0,)), ((), ()))


def dot(a, b, dims=NN):
    return lax.dot_general(a, b, dims, preferred_element_type=jnp.float32)


def in_hbm(array):
    return pltpu.with_memory_space_constraint(array, pltpu.HBM)


def swap(block, axis, mask):
    route = [(i, i ^ mask) for i in range(lax.axis_size(axis))]
    return lax.ppermute(block, axis, route)


def slots_of(ids, chips, block):
    tok = ids.shape[1]
    chip = lax.axis_index("expert") // 2
    ranks = -(-chips // 8) * 8
    apart = jnp.bitwise_xor(ids, chip)
    match = lax.broadcasted_iota(jnp.int32, (ranks, tok), 0) == apart
    onehot = match.astype(jnp.float32)
    earlier = lax.broadcasted_iota(jnp.int32, (tok, tok), 0) < lax.broadcasted_iota(
        jnp.int32, (tok, tok), 1
    )
    before = dot(onehot.astype(jnp.bfloat16), earlier.astype(jnp.float32).astype(jnp.bfloat16))
    rank = jnp.sum(before * onehot, axis=0, keepdims=True).astype(jnp.int32)
    return apart * block + rank


def column_of(row):
    tok = row.shape[1]
    eye = lax.broadcasted_iota(jnp.int32, (tok, tok), 0) == lax.broadcasted_iota(
        jnp.int32, (tok, tok), 1
    )
    return jnp.sum(jnp.where(eye, row, 0.0), axis=1, keepdims=True)


def dispatch_body(chips, block, *refs):
    sources, out_refs, held, sems = refs[:4], refs[4 : 4 + chips], refs[4 + chips : -1], refs[-1]
    fetches = [pltpu.make_async_copy(sources[n], held[n], sems.at[n]) for n in range(4)]
    for fetch in fetches:
        fetch.start()
    ids_ref, prob_ref, x_ref, dy_ref = held
    fetch_x, fetch_dy = fetches[2:]
    fetches[0].wait()
    fetches[1].wait()
    tok = x_ref.shape[0]
    slot = slots_of(ids_ref[...], chips, block)
    rows = chips * block
    placing = (lax.broadcasted_iota(jnp.int32, (rows, tok), 0) == slot).astype(jnp.float32)
    placing = placing.astype(jnp.bfloat16)
    column = column_of(prob_ref[...])
    fetch_x.wait()
    send_x = dot(placing, x_ref[...]).astype(jnp.bfloat16)
    for j in range(chips):
        out_refs[j][:block, :] = send_x[j * block : (j + 1) * block]
    fetch_dy.wait()
    scaled = (column * dy_ref[...].astype(jnp.float32)).astype(jnp.bfloat16)
    send_dy = dot(placing, scaled).astype(jnp.bfloat16)
    for j in range(chips):
        out_refs[j][block:, :] = send_dy[j * block : (j + 1) * block]


def stage_body(*refs):
    count = len(refs) // 2
    sems = refs[-1]
    copies = [pltpu.make_async_copy(refs[n], refs[count + n], sems.at[n]) for n in range(count)]
    for copy in copies:
        copy.start()
    for copy in copies:
        copy.wait()


def stage(arrays):
    return pl.pallas_call(
        stage_body,
        in_specs=[pl.BlockSpec(memory_space=pltpu.HBM)] * len(arrays),
        out_specs=[pl.BlockSpec(memory_space=pltpu.VMEM)] * len(arrays),
        out_shape=[pltpu.VMEM(a.shape, a.dtype) for a in arrays],
        scratch_shapes=[pltpu.SemaphoreType.DMA((len(arrays),))],
        compiler_params=pltpu.CompilerParams(vmem_limit_bytes=8 << 20),
        cost_estimate=pl.CostEstimate(
            flops=0, bytes_accessed=sum(4 * a.size for a in arrays), transcendentals=0
        ),
        name="stage",
    )(*[in_hbm(a) for a in arrays])


def combine_body(chips, block, ids_ref, prob_ref, *refs):
    back, (out_ref, grad_ref) = refs[:chips], refs[chips:]
    tok = out_ref.shape[0]
    slot = slots_of(ids_ref[...], chips, block)
    rows = chips * block
    placing = (lax.broadcasted_iota(jnp.int32, (rows, tok), 0) == slot).astype(jnp.float32)
    placing = placing.astype(jnp.bfloat16)
    out = jnp.concatenate([ref[:block, :] for ref in back], axis=0)
    grad = jnp.concatenate([ref[block:, :] for ref in back], axis=0)
    out_ref[...] = (column_of(prob_ref[...]) * dot(placing, out, TN)).astype(jnp.bfloat16)
    grad_ref[...] = dot(placing, grad, TN).astype(jnp.bfloat16)


def side_by_side(own, other, part):
    wide = [jnp.concatenate([own[n][0, :, part], other[n][0, :, part]], axis=1) for n in (0, 1)]
    if len(own) < 3:
        return wide
    return wide + [jnp.concatenate([own[2][0, part, :], other[2][0, part, :]], axis=0)]


def forward_body(count, block, tile, *refs):
    chunks, own, other = refs[:count], refs[count : count + 2], refs[count + 2 : count + 4]
    kept_ref, shared_ref, gate_ref, up_ref = refs[count + 4 :]
    model = chunks[0].shape[1]
    x = jnp.concatenate([ref[:block, :] for ref in chunks], axis=0)
    shared_ref[:, :model] = jnp.concatenate([ref[block:, :] for ref in chunks], axis=0)
    for first in range(0, kept_ref.shape[1], tile):
        part = slice(first, first + tile)
        gate_w, up_w = side_by_side(own, other, part)
        gate = dot(x, gate_w)
        up = dot(x, up_w)
        hidden = (gate * jax.nn.sigmoid(gate) * up).astype(jnp.bfloat16)
        kept_ref[:, part] = hidden[:, :tile]
        shared_ref[:, model + first : model + first + tile] = hidden[:, tile:]
        gate_ref[:, 2 * first : 2 * (first + tile)] = gate
        up_ref[:, 2 * first : 2 * (first + tile)] = up


def expert_body(count, block, tile, ready, *refs):
    chunks, refs = refs[:count], refs[count:]
    own, other, refs = refs[:3], refs[3:6], refs[6:]
    if ready:
        (kept_ref, shared_ref, gate_ref, up_ref), refs = refs[:4], refs[4:]
        backs, (out, grad) = refs[:count], refs[count:]
    else:
        backs, (kept_ref, shared_ref, out, grad) = refs[:count], refs[count:]
    model = chunks[0].shape[1]
    units = kept_ref.shape[1]
    dy = jnp.concatenate([ref[block:, :] for ref in chunks], axis=0)
    if not ready:
        x = jnp.concatenate([ref[:block, :] for ref in chunks], axis=0)
        shared_ref[:, :model] = dy
    for first in range(0, units, tile):
        part = slice(first, first + tile)
        gate_w, up_w, down_w = side_by_side(own, other, part)
        if ready:
            gate = gate_ref[:, 2 * first : 2 * (first + tile)]
            up = up_ref[:, 2 * first : 2 * (first + tile)]
        else:
            gate = dot(x, gate_w)
            up = dot(x, up_w)
        grad_hidden = dot(dy, down_w, NT)
        sig = jax.nn.sigmoid(gate)
        active = gate * sig
        hidden = (active * up).astype(jnp.bfloat16)
        if not ready:
            kept_ref[:, part] = hidden[:, :tile]
            shared_ref[:, model + first : model + first + tile] = hidden[:, tile:]
        grad_gate = (grad_hidden * up * sig * (1.0 + gate * (1.0 - sig))).astype(jnp.bfloat16)
        grad_up = (grad_hidden * active).astype(jnp.bfloat16)
        new_out = dot(hidden, down_w)
        new_grad = dot(grad_gate, gate_w, NT) + dot(grad_up, up_w, NT)
        if first:
            new_out, new_grad = out[...] + new_out, grad[...] + new_grad
        if first + tile < units:
            out[...], grad[...] = new_out, new_grad
            continue
        for n in range(count):
            backs[n][:block, :] = new_out[n * block : (n + 1) * block, :].astype(jnp.bfloat16)
            backs[n][block:, :] = new_grad[n * block : (n + 1) * block, :].astype(jnp.bfloat16)


def forward(chunks, own, other):
    count = len(chunks)
    block, model = chunks[0].shape[0] // 2, chunks[0].shape[1]
    units = own[0].shape[2]
    rows = count * block
    vmem = pl.BlockSpec(memory_space=pltpu.VMEM)
    return pl.pallas_call(
        functools.partial(forward_body, count, block, 128),
        in_specs=[vmem] * (count + 4),
        out_specs=[vmem] * 4,
        out_shape=[
            jax.ShapeDtypeStruct((rows, units), jnp.bfloat16),
            jax.ShapeDtypeStruct((rows, model + units), jnp.bfloat16),
            jax.ShapeDtypeStruct((rows, 2 * units), jnp.float32),
            jax.ShapeDtypeStruct((rows, 2 * units), jnp.float32),
        ],
        compiler_params=pltpu.CompilerParams(vmem_limit_bytes=28 << 20),
        cost_estimate=pl.CostEstimate(
            flops=8 * rows * model * units,
            bytes_accessed=8 * model * units + 4 * rows * model,
            transcendentals=2 * rows * units,
        ),
        name="forward",
    )(*chunks, *own[:2], *other[:2])


def expert(chunks, own, other, ready=()):
    count = len(chunks)
    block, model = chunks[0].shape[0] // 2, chunks[0].shape[1]
    units = own[0].shape[2]
    rows = count * block
    vmem = pl.BlockSpec(memory_space=pltpu.VMEM)
    out_shape = [jax.ShapeDtypeStruct((2 * block, model), jnp.bfloat16)] * count
    if not ready:
        out_shape += [
            jax.ShapeDtypeStruct((rows, units), jnp.bfloat16),
            jax.ShapeDtypeStruct((rows, model + units), jnp.bfloat16),
        ]
    results = pl.pallas_call(
        functools.partial(expert_body, count, block, 128, bool(ready)),
        in_specs=[vmem] * (count + 6 + len(ready)),
        out_specs=[vmem] * len(out_shape),
        out_shape=out_shape,
        scratch_shapes=[
            pltpu.VMEM((rows, model), jnp.float32),
            pltpu.VMEM((rows, model), jnp.float32),
        ],
        compiler_params=pltpu.CompilerParams(vmem_limit_bytes=28 << 20),
        cost_estimate=pl.CostEstimate(
            flops=(16 if ready else 24) * rows * model * units,
            bytes_accessed=12 * model * units + 8 * rows * model,
            transcendentals=2 * rows * units,
        ),
        name="expert",
    )(*chunks, *own, *other, *ready)
    return results[:count], results[count:]


def weight_body(chunk_count, groups, block, parts, *refs):
    chunks, kept = refs[:chunk_count], refs[chunk_count : chunk_count + groups]
    shared = refs[chunk_count + groups : chunk_count + 2 * groups]
    outs, term = refs[chunk_count + 2 * groups : -1], refs[-1]
    columns = term.shape[1]
    model = chunks[0].shape[1]
    here = pl.ds(pl.multiple_of(pl.program_id(0) * columns, columns), columns)
    hidden = jnp.concatenate(
        [ref[...] for ref in kept] + [ref[:, model:] for ref in shared], axis=0
    )
    dy = jnp.concatenate(
        [ref[block:, here] for ref in chunks] + [ref[:, here] for ref in shared], axis=0
    )
    term[...] = dot(hidden, dy, TN)
    if parts == 1:
        outs[0][...] = term[...].astype(jnp.bfloat16)
        return
    me = lax.axis_index("dp")
    height = term.shape[0] // parts
    for m in range(parts):
        first = pl.multiple_of(jnp.bitwise_xor(me, m) * height, 8)
        outs[m][...] = term[pl.ds(first, height), :].astype(jnp.bfloat16)


def weight_terms(chunks, kept, shared, parts):
    block, model = chunks[0].shape[0] // 2, chunks[0].shape[1]
    units = kept[0].shape[1]
    columns = 512
    full = lambda a: pl.BlockSpec(a.shape, lambda i: (0, 0))
    rows = 2 * sum(a.shape[0] for a in kept)
    return pl.pallas_call(
        functools.partial(weight_body, len(chunks), len(kept), block, parts),
        grid=(model // columns,),
        in_specs=[full(a) for a in (*chunks, *kept, *shared)],
        out_specs=[pl.BlockSpec((units // parts, columns), lambda i: (0, i))] * parts,
        out_shape=[jax.ShapeDtypeStruct((units // parts, model), jnp.bfloat16)] * parts,
        scratch_shapes=[pltpu.VMEM((units, columns), jnp.float32)],
        compiler_params=pltpu.CompilerParams(vmem_limit_bytes=16 << 20),
        cost_estimate=pl.CostEstimate(
            flops=2 * rows * model * units,
            bytes_accessed=2 * (rows * (model + units) + units * model),
            transcendentals=0,
        ),
        name="weight_terms",
    )(*chunks, *kept, *shared)


def add_body(*refs):
    total = refs[0][...].astype(jnp.float32)
    for ref in refs[1:-1]:
        total = total + ref[...].astype(jnp.float32)
    refs[-1][...] = total.astype(jnp.bfloat16)


def add_terms(terms):
    return pl.pallas_call(
        add_body,
        out_shape=jax.ShapeDtypeStruct(terms[0].shape, jnp.bfloat16),
        compiler_params=pltpu.CompilerParams(vmem_limit_bytes=8 << 20),
        cost_estimate=pl.CostEstimate(
            flops=len(terms) * terms[0].size,
            bytes_accessed=2 * (len(terms) + 1) * terms[0].size,
            transcendentals=0,
        ),
        name="add_terms",
    )(*terms)


def plan(chips):
    each = max(1, chips // 4)
    groups = [list(range(g, g + each)) for g in range(0, chips, each)]
    if len(groups) > 1:
        groups = groups[:2:-1] + [groups[0] + groups[1]] + groups[2:3]
    return [j for group in groups for j in group if j], groups


def direct_sum(parts, units):
    return parts <= 8 and units % (8 * parts) == 0


def per_device(tokens_in, cotangent, router_prob, expert_ids, w_gate, w_up, w_down):
    chips = lax.axis_size("expert") // 2
    tok, model = tokens_in.shape
    most = 5 * tok // (4 * chips)
    block = -(-most // 8) * 8
    ids = expert_ids.reshape(1, tok)
    prob = router_prob.reshape(1, tok)
    sends = pl.pallas_call(
        functools.partial(dispatch_body, chips, block),
        in_specs=[pl.BlockSpec(memory_space=pltpu.HBM)] * 4,
        out_shape=[jax.ShapeDtypeStruct((2 * block, model), jnp.bfloat16)] * chips,
        scratch_shapes=[
            pltpu.VMEM((1, tok), jnp.int32),
            pltpu.VMEM((1, tok), jnp.float32),
            pltpu.VMEM((tok, model), jnp.bfloat16),
            pltpu.VMEM((tok, model), jnp.bfloat16),
            pltpu.SemaphoreType.DMA((4,)),
        ],
        compiler_params=pltpu.CompilerParams(vmem_limit_bytes=16 << 20),
        cost_estimate=pl.CostEstimate(
            flops=4 * chips * block * tok * model,
            bytes_accessed=4 * (chips * block + tok) * model,
            transcendentals=0,
        ),
        name="dispatch",
    )(*[in_hbm(a) for a in (ids, prob, tokens_in, cotangent)])
    own = (w_gate, w_up, w_down)
    order, groups = plan(chips)
    arrived = {0: sends[0]}
    for j in order:
        arrived[j] = swap(sends[j], "expert", 2 * j)
    other = tuple(swap(w, "expert", 1) for w in own)
    own = stage(own)
    kept, shared, backs = [], [], {}
    for g, group in enumerate(groups):
        chunks = [arrived[j] for j in group]
        if g == len(groups) - 1:
            saved = forward(chunks, own, other)
        else:
            results, saved = expert(chunks, own, other)
            for j, result in zip(group, results):
                backs[j] = swap(result, "expert", 2 * j) if j else result
        kept.append(saved[0])
        shared.append(swap(saved[1], "expert", 1))
    results, _ = expert(chunks, own, other, saved)
    for j, result in zip(groups[-1], results):
        backs[j] = swap(result, "expert", 2 * j) if j else result
    parts = lax.axis_size("dp")
    direct = direct_sum(parts, w_down.shape[1])
    rows = [arrived[j] for group in groups for j in group]
    terms = weight_terms(rows, kept, shared, parts if direct else 1)
    if direct:
        spread = [swap(terms[m], "dp", m) for m in range(1, parts)]
        summed = add_terms([terms[0], *spread])
    else:
        summed = lax.psum_scatter(terms[0], "dp", scatter_dimension=0, tiled=True)
    layer_out, grad_input = pl.pallas_call(
        functools.partial(combine_body, chips, block),
        out_shape=[jax.ShapeDtypeStruct((tok, model), jnp.bfloat16)] * 2,
        compiler_params=pltpu.CompilerParams(vmem_limit_bytes=16 << 20),
        cost_estimate=pl.CostEstimate(
            flops=4 * chips * block * tok * model,
            bytes_accessed=4 * (chips * block + tok) * model,
            transcendentals=0,
        ),
        name="combine",
    )(ids, prob, *[backs[j] for j in range(chips)])
    return layer_out, grad_input, summed[None]


def solution(mesh):
    placed = (
        P(("dp", "expert"), None),
        P(("dp", "expert"), None),
        P(("dp", "expert")),
        P(("dp", "expert"), None),
        P("expert", None, None),
        P("expert", None, None),
        P("expert", None, None),
    )

    return jax.shard_map(
        per_device,
        mesh=mesh,
        in_specs=placed,
        out_specs=(P(("dp", "expert"), None), P(("dp", "expert"), None), P("expert", "dp", None)),
        check_vma=False,
    )
```
